32 devices in a mesh: seq: 16 (over z, x, core), exp: 2 (over y).
Axes of the slice: x: 2, y: 2, z: 4, core: 2. Of those that a mesh axis runs over, the one named last changes fastest.
Arguments:
- tokens: bfloat16 [30720, 1024], P('seq'), may hold values from -24 to 24
- slot_embed: bfloat16 [1024, 512], P(None, 'exp'), may hold values from -3 to 3
- w_in: bfloat16 [32, 1024, 4096], P('exp', None, 'seq'), may hold values from -0.375 to 0.375
- w_out: bfloat16 [32, 4096, 1024], P('exp', 'seq'), may hold values from -0.125 to 0.125
Outputs:
- mixed_out: bfloat16 [30720, 1024], P('seq', 'exp')
The draws below stay inside these ranges and needn't reach their ends.
All inputs are finite; a program needn't handle non-finite values.
Results may differ from the reference program's by a relative error of at most 0.012.
Values may be sent and summed in bfloat16 or wider, within the bound.
A program may use at most 64 MiB of HBM per device.

```python
import math
import jax
import jax.numpy as jnp
from jax import lax

D = 1024
HID = 4096
SLOT_EXP = 16
TOK_DEV = 1920
TOKENS = 30720
EXPERTS = 32
SLOTS = 512
N_SEQ = 16
N_EXP = 2


def embed_table(key):
    fraction = jnp.arange(SLOTS, dtype=jnp.float32) / max(SLOTS - 1, 1)
    base_scale = 3.0 / math.sqrt(D) * (0.9 + 0.25 * fraction)
    normals = jnp.clip(jax.random.normal(jax.random.fold_in(key, 11), (D, SLOTS), jnp.float32), -6.0, 6.0)
    table = normals * base_scale[None, :]
    return table


def draw_slot_embed(key, part):
    table = embed_table(key)
    return table.astype(jnp.bfloat16)


def draw_tokens(key, part):
    position = jnp.arange(TOKENS, dtype=jnp.float32) / max(TOKENS - 1, 1)
    row_scale = 0.9 + 0.2 * position
    entries = jnp.clip(jax.random.normal(jax.random.fold_in(key, 21), (TOKENS, D), jnp.float32), -6.0, 6.0)
    values = entries * row_scale[:, None]
    return values.astype(jnp.bfloat16)


def steps_of(key, extent, pieces, low, top_value):
    level = 1.0
    for axis_at, shards_of in pieces:
        draws = jax.random.uniform(jax.random.fold_in(jax.random.fold_in(key, 6), axis_at), (shards_of,), jnp.float32, low / len(pieces), top_value / len(pieces))
        level = level * jnp.repeat(jnp.exp(draws), extent[axis_at] // shards_of).reshape((-1,) + (1,) * (len(extent) - 1 - axis_at))
    return level


def scatter_about(own_key, shape, width, reach, pieces=(), kind=jnp.bfloat16):
    factor_of = steps_of(own_key, shape, pieces, -0.22, 0.18) if pieces else 1.0
    values = jax.random.normal(own_key, shape, jnp.float32) * width * factor_of
    return jnp.minimum(jnp.maximum(values, -reach), reach).astype(kind)


def setup_inputs(seed: int = 0) -> dict:
    keys = jax.random.split(jax.random.key(seed), 5)
    return {
        "tokens": draw_tokens(jax.random.fold_in(keys[4], 71), 0),
        "slot_embed": draw_slot_embed(jax.random.fold_in(keys[4], 71), 0),
        "w_in": scatter_about(keys[2], (EXPERTS, D, HID), (D // 4) ** -0.5, 0.375, ((0, 2), (2, 16))),
        "w_out": scatter_about(keys[3], (EXPERTS, HID, D), (HID // 2) ** -0.5, 0.125, ((0, 2), (1, 16))),
    }


def gelu_tanh(values):
    return 0.5 * values * (1.0 + jnp.tanh(0.7978845608028654 * (values + 0.044715 * values * values * values)))


def reference(tokens, slot_embed, w_in, w_out):
    group_size = SLOTS // N_EXP
    blocks = slot_embed.reshape(D, N_EXP, group_size).transpose(1, 0, 2)

    def dispatch_block(embed_block):
        logits = jnp.dot(tokens, embed_block, preferred_element_type=jnp.float32)
        col_peak = jnp.max(logits, axis=0)
        weights = jnp.exp(logits - col_peak[None, :])
        col_total = jnp.sum(weights, axis=0)
        dispatch = (weights / col_total[None, :]).astype(jnp.bfloat16)
        summed = lax.dot_general(dispatch, tokens, (((0,), (0,)), ((), ())), preferred_element_type=jnp.float32)
        return summed.astype(jnp.bfloat16)

    slot_in = lax.map(dispatch_block, blocks).reshape(EXPERTS, SLOT_EXP, D)

    def expert_apply(operands):
        inputs, first, second = operands
        hidden = gelu_tanh(jnp.dot(inputs, first, preferred_element_type=jnp.float32)).astype(jnp.bfloat16)
        return jnp.dot(hidden, second, preferred_element_type=jnp.float32).astype(jnp.bfloat16)

    slot_out = lax.map(expert_apply, (slot_in, w_in, w_out)).reshape(N_EXP, group_size, D)
    row_blocks = tokens.reshape(N_SEQ, TOK_DEV, D)

    def combine_block(row_block):
        logits = jnp.dot(row_block, slot_embed, preferred_element_type=jnp.float32)
        row_peak = jnp.max(logits, axis=1)
        weights = jnp.exp(logits - row_peak[:, None])
        row_total = jnp.sum(weights, axis=1)
        combine = (weights / row_total[:, None]).astype(jnp.bfloat16)
        part_blocks = combine.reshape(TOK_DEV, N_EXP, group_size).astype(jnp.float32)
        group_mix = jnp.einsum("bgs,gsd->bgd", part_blocks, slot_out.astype(jnp.float32)).astype(jnp.bfloat16)
        group_mix = lax.optimization_barrier(group_mix)
        return jnp.sum(group_mix.astype(jnp.float32), axis=1).astype(jnp.bfloat16)

    return lax.map(combine_block, row_blocks).reshape(TOKENS, D)
```

```python
import functools

import jax
import jax.numpy as jnp
from jax import lax
from jax.experimental import pallas as pl
from jax.experimental.pallas import tpu as pltpu
from jax.sharding import PartitionSpec as P

MESH = pl.DeviceIdType.MESH
F32 = jnp.float32
BF16 = jnp.bfloat16


def gelu_tanh(v):
    return 0.5 * v * (1.0 + jnp.tanh(0.7978845608028654 * (v + 0.044715 * v * v * v)))


def rcopy(src, dst, send, recv, dev):
    return pltpu.make_async_remote_copy(
        src_ref=src, dst_ref=dst, send_sem=send, recv_sem=recv, device_id=dev, device_id_type=MESH
    )


def column(row, slots):
    return jnp.transpose(jnp.broadcast_to(row, (128, slots)))


def kernel(
    n_seq, n_exp, slot_exp, tok_hbm, emb_hbm, win_hbm, wout_hbm, comb_hbm, so_hbm,
    tok, emb, embt, win, wout, logt, pt, acc, comb, mst, lst, tot,
    snd1, rcv1, snd2, rcv2, ag, keep, snd3, rcv3, snd4, rcv4, ybuf, so,
    sem_tok, sem_in, sem_w, sem_out, sem_emb, sem_m, sem_l,
    sem_1, sem_2, sem_ag, sem_fw, sem_3, sem_4, sem_y, sem_a, sem_af, sem_b, sem_bf,
):
    n_chip = n_seq // 2
    count, features = tok.shape
    slots = embt.shape[0]
    experts = win.shape[0]
    rows = slots // n_seq
    half = slots // 2
    cols = features // n_exp
    tile = 256
    n_tile = features // tile
    me = lax.axis_index("seq")
    mine = lax.axis_index("exp")
    chip = me // 2
    core = lax.rem(me, 2)
    other = 1 - core
    partner = {"seq": chip * 2 + other}
    pending = []

    def chip_at(r):
        return lax.rem(chip + r, n_chip)

    def chip_from(r):
        return lax.rem(chip - r + n_chip, n_chip)

    def seq_at(r):
        return {"seq": lax.rem(me + r, n_seq)}

    def exp_at(r):
        return {"exp": lax.rem(mine + r, n_exp)}

    def go(cp):
        cp.start()
        pending.append(cp)

    barrier = pltpu.get_barrier_semaphore()
    for r in range(1, n_seq):
        pl.semaphore_signal(barrier, inc=1, device_id=seq_at(r), device_id_type=MESH)
    for r in range(1, n_exp):
        pl.semaphore_signal(barrier, inc=1, device_id=exp_at(r), device_id_type=MESH)

    emb_in = pltpu.make_async_copy(emb_hbm, emb.at[0], sem_in)
    emb_in.start()
    chunks = []
    at = 0
    while at < count:
        size = min(512, count - at)
        cp = pltpu.make_async_copy(tok_hbm.at[pl.ds(at, size)], tok.at[pl.ds(at, size)], sem_tok.at[len(chunks)])
        cp.start()
        chunks.append((at, size, cp))
        at += size
    win_in = pltpu.make_async_copy(win_hbm, win, sem_w.at[0])
    wout_in = pltpu.make_async_copy(wout_hbm, wout, sem_w.at[1])
    win_in.start()
    wout_in.start()

    emb_in.wait()
    for q in range(n_tile):
        embt[:, q * tile:(q + 1) * tile] = jnp.transpose(emb[0, q * tile:(q + 1) * tile, :])
    peak = None
    for at, size, cp in chunks:
        cp.wait()
        lt = lax.dot_general(
            embt[...], tok[at:at + size, :], (((1,), (1,)), ((), ())), preferred_element_type=F32
        )
        logt[:, at:at + size] = lt
        top = jnp.max(lt, axis=1, keepdims=True)
        peak = top if peak is None else jnp.maximum(peak, top)
    peak_wide = jnp.broadcast_to(peak, (slots, 128))
    mst[0] = jnp.transpose(peak_wide)[0:8, :]

    pl.semaphore_wait(barrier, n_seq - 1 + n_exp - 1)
    stat_m = [rcopy(mst.at[0], mst.at[r], sem_m.at[0, r], sem_m.at[1, r], seq_at(r)) for r in range(1, n_seq)]
    for cp in stat_m:
        go(cp)
    embs = [rcopy(emb.at[0], emb.at[r], sem_emb.at[0, r], sem_emb.at[1, r], exp_at(r)) for r in range(1, n_exp)]
    for cp in embs:
        go(cp)

    total = None
    for at, size, _ in chunks:
        w = jnp.exp(logt[:, at:at + size] - peak)
        pt[:, at:at + size] = w.astype(BF16)
        part = jnp.sum(w, axis=1, keepdims=True)
        total = part if total is None else total + part
    lst[0] = jnp.transpose(jnp.broadcast_to(total, (slots, 128)))[0:8, :]
    stat_l = [rcopy(lst.at[0], lst.at[r], sem_l.at[0, r], sem_l.at[1, r], seq_at(r)) for r in range(1, n_seq)]
    for cp in stat_l:
        go(cp)

    for q in range(n_tile):
        acc[:, q * tile:(q + 1) * tile] = jnp.dot(
            pt[...], tok[:, q * tile:(q + 1) * tile], preferred_element_type=F32
        )
    for cp in stat_m:
        cp.wait_recv()
    top_all = jnp.max(mst[...], axis=0)
    scale = column(jnp.exp(mst[0] - top_all)[0:1, :], slots)[:, 0:1]

    def half_rows(which):
        return pl.ds(pl.multiple_of(which * half, half), half)

    acc[...] = acc[...] * scale
    first = []
    for q in range(n_tile):
        snd1[q] = acc[half_rows(other), q * tile:(q + 1) * tile].astype(BF16)
        cp = rcopy(snd1.at[q], rcv1.at[q], sem_1.at[0, q], sem_1.at[1, q], partner)
        go(cp)
        first.append(cp)
    for q in range(n_tile):
        first[q].wait_recv()
        both = acc[half_rows(core), q * tile:(q + 1) * tile] + rcv1[q].astype(F32)
        snd2[:, :, q * tile:(q + 1) * tile] = both.reshape(n_chip, rows, tile).astype(BF16)
    second = []
    for r in range(1, n_chip):
        to = chip_at(r)
        cp = rcopy(snd2.at[to], rcv2.at[r], sem_2.at[0, r], sem_2.at[1, r], {"seq": to * 2 + core})
        go(cp)
        second.append(cp)

    for cp in embs:
        cp.wait_recv()
    step = next(s for s in (384, 256, 128, 64, 32, 16) if count % s == 0)

    def combine(i, carry):
        here = pl.ds(pl.multiple_of(i * step, step), step)
        rows_in = tok[here, :]
        parts = [jnp.dot(rows_in, emb[r], preferred_element_type=F32) for r in range(n_exp)]
        top = jnp.max(functools.reduce(jnp.maximum, parts), axis=1, keepdims=True)
        parts = [jnp.exp(v - top) for v in parts]
        full = jnp.sum(functools.reduce(jnp.add, parts), axis=1, keepdims=True)
        inv = 1.0 / full
        for r in range(n_exp):
            comb[here, r * slots:(r + 1) * slots] = (parts[r] * inv).astype(BF16)
        return carry

    lax.fori_loop(0, count // step, combine, 0)
    comb_out = pltpu.make_async_copy(comb, comb_hbm, sem_out.at[0])
    comb_out.start()

    for cp in stat_l:
        cp.wait_recv()
    grand = jnp.sum(lst[...] * jnp.exp(mst[...] - top_all[None]), axis=0)
    tot[...] = column(grand[0:1, :], slots)
    piece = core * n_chip + chip
    mine_sum = snd2[chip].astype(F32)
    for r in range(1, n_chip):
        second[r - 1].wait_recv()
        mine_sum = mine_sum + rcv2[r].astype(F32)
    total_here = tot[pl.ds(pl.multiple_of(piece * rows, rows), rows), :][:, 0:1]
    ag[piece] = (mine_sum / total_here).astype(BF16)

    for r in range(1, n_chip):
        go(rcopy(ag.at[piece], ag.at[piece], sem_ag.at[0, r], sem_ag.at[1, r], {"seq": chip_at(r) * 2 + core}))
    go(rcopy(ag.at[piece], ag.at[piece], sem_fw.at[0, 0], sem_fw.at[1, 0], partner))
    win_in.wait()
    wout_in.wait()

    def expert(p):
        e = (p * rows) // slot_exp
        h = gelu_tanh(jnp.dot(ag[p], win[e], preferred_element_type=F32)).astype(BF16)
        return jnp.dot(h, wout[e], preferred_element_type=F32)

    group = 4
    for start in range(0, n_chip, group):
        rs = range(start, start + group)
        for r in rs:
            p = core * n_chip + chip_from(r)
            if r:
                rcopy(ag.at[p], ag.at[p], sem_ag.at[0, r], sem_ag.at[1, r], partner).wait_recv()
                go(rcopy(ag.at[p], ag.at[p], sem_fw.at[0, r], sem_fw.at[1, r], partner))
        for r in rs:
            keep[chip_from(r)] = expert(core * n_chip + chip_from(r))
    for start in range(0, n_chip, group):
        rs = range(start, start + group)
        for r in rs:
            p = other * n_chip + chip_from(r)
            rcopy(ag.at[p], ag.at[p], sem_fw.at[0, r], sem_fw.at[1, r], partner).wait_recv()
        for r in rs:
            snd3[r] = expert(other * n_chip + chip_from(r)).astype(BF16)
        for r in rs:
            go(rcopy(snd3.at[r], rcv3.at[r], sem_3.at[0, r], sem_3.at[1, r], partner))
    for r in range(n_chip):
        rcopy(snd3.at[r], rcv3.at[r], sem_3.at[0, r], sem_3.at[1, r], partner).wait_recv()
        owner = chip_from(r)
        snd4[r] = (keep[owner] + rcv3[r].astype(F32)).astype(BF16)
        if r:
            go(rcopy(snd4.at[r], rcv4.at[r], sem_4.at[0, r], sem_4.at[1, r], {"seq": owner * 2 + core}))
    final = snd4[0].astype(F32)
    for r in range(1, n_chip):
        rcopy(snd4.at[r], rcv4.at[r], sem_4.at[0, r], sem_4.at[1, r], partner).wait_recv()
        final = final + rcv4[r].astype(F32)
    final = final.astype(BF16)
    for q in range(n_exp):
        ybuf[q] = final[:, q * cols:(q + 1) * cols]
    for r in range(1, n_exp):
        go(rcopy(ybuf.at[lax.rem(mine + r, n_exp)], so.at[r, piece], sem_y.at[0, r], sem_y.at[1, r], exp_at(r)))
    so[0, piece] = ybuf[mine]

    def spread(span, sem_d, sem_r):
        def at_piece(p):
            return so.at[span, p]

        for r in range(1, n_chip):
            go(rcopy(at_piece(piece), at_piece(piece), sem_d.at[0, r], sem_d.at[1, r], {"seq": chip_at(r) * 2 + core}))
        go(rcopy(at_piece(piece), at_piece(piece), sem_r.at[0, 0], sem_r.at[1, 0], partner))

    def relay(span, sem_d, sem_r):
        for r in range(1, n_chip):
            p = core * n_chip + chip_from(r)
            rcopy(so.at[span, p], so.at[span, p], sem_d.at[0, r], sem_d.at[1, r], partner).wait_recv()
            go(rcopy(so.at[span, p], so.at[span, p], sem_r.at[0, r], sem_r.at[1, r], partner))

    def finish(span, sem_r):
        for r in range(n_chip):
            p = other * n_chip + chip_from(r)
            rcopy(so.at[span, p], so.at[span, p], sem_r.at[0, r], sem_r.at[1, r], partner).wait_recv()

    near = pl.ds(0, 1)
    far = pl.ds(1, n_exp - 1)
    spread(near, sem_a, sem_af)
    for r in range(1, n_exp):
        rcopy(ybuf.at[0], so.at[r, piece], sem_y.at[0, r], sem_y.at[1, r], exp_at(r)).wait_recv()
    spread(far, sem_b, sem_bf)
    relay(near, sem_a, sem_af)
    relay(far, sem_b, sem_bf)
    finish(near, sem_af)
    finish(far, sem_bf)
    so_out = pltpu.make_async_copy(so, so_hbm, sem_out.at[1])
    so_out.start()
    for cp in pending:
        cp.wait_send()
    comb_out.wait()
    so_out.wait()


def solution(mesh):
    n_seq, n_exp = mesh.shape["seq"], mesh.shape["exp"]
    n_chip = n_seq // 2

    def on_device(tokens, slot_embed, w_in, w_out):
        count, features = tokens.shape
        slots = slot_embed.shape[1]
        experts, _, hid = w_in.shape
        slot_exp = slots // experts
        rows = slots // n_seq
        half = slots // 2
        cols = features // n_exp
        n_tile = features // 256
        dma = pltpu.SemaphoreType.DMA
        vmem = pltpu.VMEM
        anywhere = pl.BlockSpec(memory_space=pl.ANY)
        comb, so = pl.pallas_call(
            functools.partial(kernel, n_seq, n_exp, slot_exp),
            out_shape=(
                jax.ShapeDtypeStruct((count, n_exp * slots), BF16),
                jax.ShapeDtypeStruct((n_exp, n_seq, rows, cols), BF16),
            ),
            in_specs=[anywhere] * 4,
            out_specs=(anywhere, anywhere),
            scratch_shapes=[
                vmem((count, features), BF16),
                vmem((n_exp, features, slots), BF16),
                vmem((slots, features), BF16),
                vmem(w_in.shape, BF16),
                vmem(w_out.shape, BF16),
                vmem((slots, count), F32),
                vmem((slots, count), BF16),
                vmem((slots, features), F32),
                vmem((count, n_exp * slots), BF16),
                vmem((n_seq, 8, slots), F32),
                vmem((n_seq, 8, slots), F32),
                vmem((slots, 128), F32),
                vmem((n_tile, half, 256), BF16),
                vmem((n_tile, half, 256), BF16),
                vmem((n_chip, rows, features), BF16),
                vmem((n_chip, rows, features), BF16),
                vmem((n_seq, rows, features), BF16),
                vmem((n_chip, rows, features), F32),
                vmem((n_chip, rows, features), BF16),
                vmem((n_chip, rows, features), BF16),
                vmem((n_chip, rows, features), BF16),
                vmem((n_chip, rows, features), BF16),
                vmem((n_exp, rows, cols), BF16),
                vmem((n_exp, n_seq, rows, cols), BF16),
                dma((-(-count // 512),)),
                dma,
                dma((2,)),
                dma((2,)),
                dma((2, n_exp)),
                dma((2, n_seq)),
                dma((2, n_seq)),
                dma((2, n_tile)),
                dma((2, n_chip)),
                dma((2, n_chip)),
                dma((2, n_chip)),
                dma((2, n_chip)),
                dma((2, n_chip)),
                dma((2, n_exp)),
                dma((2, n_chip)),
                dma((2, n_chip)),
                dma((2, n_chip)),
                dma((2, n_chip)),
            ],
            compiler_params=pltpu.CompilerParams(
                collective_id=0, has_side_effects=True, vmem_limit_bytes=60 * 1024 * 1024
            ),
        )(tokens, slot_embed, w_in, w_out)
        so = so.reshape(n_exp * slots, cols)
        return jnp.dot(comb, so, preferred_element_type=F32).astype(BF16)

    placed = (P("seq", None), P(None, "exp"), P("exp", None, "seq"), P("exp", "seq", None))
    return jax.shard_map(
        on_device, mesh=mesh, in_specs=placed, out_specs=P("seq", "exp"), check_vma=False
    )
```

```python
import functools

import jax
import jax.numpy as jnp
from jax import lax
from jax.experimental import pallas as pl
from jax.experimental.pallas import tpu as pltpu
from jax.sharding import PartitionSpec as P

MESH = pl.DeviceIdType.MESH
F32 = jnp.float32
BF16 = jnp.bfloat16


def gelu_tanh(v):
    return 0.5 * v * (1.0 + jnp.tanh(0.7978845608028654 * (v + 0.044715 * v * v * v)))


def rcopy(src, dst, send, recv, dev):
    return pltpu.make_async_remote_copy(
        src_ref=src, dst_ref=dst, send_sem=send, recv_sem=recv, device_id=dev, device_id_type=MESH
    )


def column(row, slots):
    return jnp.transpose(jnp.broadcast_to(row, (128, slots)))


def kernel(
    n_seq, n_exp, slot_exp, tok_hbm, emb_hbm, win_hbm, wout_hbm, comb_hbm, so_hbm,
    tok, emb, embt, win, wout, logt, pt, acc, comb, m1, l1, s2, wide, tot,
    snd1, rcv1, snd2, rcv2, ag, keep, snd3, rcv3, snd4, rcv4, so,
    sem_tok, sem_in, sem_w, sem_out, sem_emb, sem_er, sem_m, sem_s,
    sem_1, sem_2, sem_ag, sem_fw, sem_3, sem_4, sem_a, sem_af,
):
    n_chip = n_seq // 2
    count, features = tok.shape
    slots = embt.shape[0]
    rows = slots // n_seq
    half = slots // 2
    cols = features // n_exp
    tile = 256
    n_tile = features // tile
    me = lax.axis_index("seq")
    mine = lax.axis_index("exp")
    chip = me // 2
    core = lax.rem(me, 2)
    other = 1 - core
    partner = {"seq": chip * 2 + other}
    pending = []

    def near(r):
        return chip_ids[r]

    chip_ids = [chip]
    for r in range(1, n_chip):
        mate, bit = chip, 1
        while bit < n_chip:
            if r & bit:
                mate = mate + bit * (1 - 2 * lax.rem(chip // bit, 2))
            bit *= 2
        chip_ids.append(mate)

    def peer(r):
        return {"seq": near(r) * 2 + core}

    def group_at(s):
        return lax.rem(mine + s, n_exp)

    def across(r, s):
        return {"seq": near(r) * 2 + core, "exp": group_at(s)}

    def go(cp):
        cp.start()
        pending.append(cp)

    barrier = pltpu.get_barrier_semaphore()
    for s in range(n_exp):
        for r in range(n_chip):
            if r or s:
                pl.semaphore_signal(barrier, inc=1, device_id=across(r, s), device_id_type=MESH)
    pl.semaphore_signal(barrier, inc=1, device_id=partner, device_id_type=MESH)

    emb_in = pltpu.make_async_copy(emb_hbm, emb.at[0], sem_in)
    emb_in.start()
    chunks = []
    at = 0
    while at < count:
        size = min(512, count - at)
        cp = pltpu.make_async_copy(tok_hbm.at[pl.ds(at, size)], tok.at[pl.ds(at, size)], sem_tok.at[len(chunks)])
        cp.start()
        chunks.append((at, size, cp))
        at += size

    emb_in.wait()
    for q in range(n_tile):
        embt[:, q * tile:(q + 1) * tile] = jnp.transpose(emb[0, q * tile:(q + 1) * tile, :])
    peak = None
    deep = features // 2

    def part_of(which):
        return pl.ds(pl.multiple_of(which * deep, deep), deep)

    def emb_copy(r):
        there = emb.at[r, part_of(core)]
        return rcopy(emb.at[0, part_of(core)], there, sem_emb.at[0, r], sem_emb.at[1, r], {"exp": group_at(r)})

    def emb_relay(r, which):
        there = emb.at[r, part_of(which)]
        return rcopy(there, there, sem_er.at[0, r], sem_er.at[1, r], partner)

    for at, size, cp in chunks:
        cp.wait()
        lt = lax.dot_general(
            embt[...], tok[at:at + size, :], (((1,), (1,)), ((), ())), preferred_element_type=F32
        )
        logt[:, at:at + size] = lt
        top = jnp.max(lt, axis=1, keepdims=True)
        peak = top if peak is None else jnp.maximum(peak, top)
        if at == 0:
            pl.semaphore_wait(barrier, n_chip * n_exp)
            for r in range(1, n_exp):
                go(emb_copy(r))
    win_in = pltpu.make_async_copy(win_hbm, win, sem_w.at[0])
    wout_in = pltpu.make_async_copy(wout_hbm, wout, sem_w.at[1])
    win_in.start()
    wout_in.start()
    m1[0] = jnp.transpose(jnp.broadcast_to(peak, (slots, 128)))[0:1, :]
    m_copy = rcopy(m1.at[0], m1.at[1], sem_m.at[0, 0], sem_m.at[1, 0], partner)
    go(m_copy)

    total = None
    for at, size, _ in chunks:
        w = jnp.exp(logt[:, at:at + size] - peak)
        pt[:, at:at + size] = w.astype(BF16)
        part = jnp.sum(w, axis=1, keepdims=True)
        total = part if total is None else total + part
    l1[0] = jnp.transpose(jnp.broadcast_to(total, (slots, 128)))[0:1, :]
    l_copy = rcopy(l1.at[0], l1.at[1], sem_m.at[0, 1], sem_m.at[1, 1], partner)
    go(l_copy)

    m_copy.wait_recv()
    top_pair = jnp.maximum(m1[0], m1[1])
    scale = column(jnp.exp(m1[0] - top_pair), slots)[:, 0:1]

    def half_rows(which):
        return pl.ds(pl.multiple_of(which * half, half), half)

    first = []
    for q in range(n_tile):
        acc[:, q * tile:(q + 1) * tile] = scale * jnp.dot(
            pt[...], tok[:, q * tile:(q + 1) * tile], preferred_element_type=F32
        )
        snd1[q] = acc[half_rows(other), q * tile:(q + 1) * tile].astype(BF16)
        cp = rcopy(snd1.at[q], rcv1.at[q], sem_1.at[0, q], sem_1.at[1, q], partner)
        go(cp)
        first.append(cp)
    l_copy.wait_recv()
    s2[0, 0] = top_pair
    s2[0, 1] = l1[0] * jnp.exp(m1[0] - top_pair) + l1[1] * jnp.exp(m1[1] - top_pair)
    stats = [rcopy(s2.at[0], s2.at[r], sem_s.at[0, r], sem_s.at[1, r], peer(r)) for r in range(1, n_chip)]
    for cp in stats:
        go(cp)
    for q in range(n_tile):
        first[q].wait_recv()
        both = acc[half_rows(core), q * tile:(q + 1) * tile] + rcv1[q].astype(F32)
        snd2[:, :, q * tile:(q + 1) * tile] = both.reshape(n_chip, rows, tile).astype(BF16)
    second = []
    for r in range(1, n_chip):
        cp = rcopy(snd2.at[near(r)], rcv2.at[r], sem_2.at[0, r], sem_2.at[1, r], peer(r))
        go(cp)
        second.append(cp)

    for r in range(1, n_exp):
        emb_copy(r).wait_recv()
        go(emb_relay(r, core))
    for r in range(1, n_exp):
        emb_relay(r, other).wait_recv()
    step = next(s for s in (384, 256, 128, 64, 32, 16) if count % s == 0)

    def combine(i, carry):
        here = pl.ds(pl.multiple_of(i * step, step), step)
        rows_in = tok[here, :]
        parts = [jnp.dot(rows_in, emb[r], preferred_element_type=F32) for r in range(n_exp)]
        top = jnp.max(functools.reduce(jnp.maximum, parts), axis=1, keepdims=True)
        parts = [jnp.exp(v - top) for v in parts]
        full = jnp.sum(functools.reduce(jnp.add, parts), axis=1, keepdims=True)
        inv = 1.0 / full
        for r in range(n_exp):
            comb[here, r * slots:(r + 1) * slots] = (parts[r] * inv).astype(BF16)
        return carry

    lax.fori_loop(0, count // step, combine, 0)
    comb_out = pltpu.make_async_copy(comb, comb_hbm, sem_out.at[0])
    comb_out.start()

    for cp in stats:
        cp.wait_recv()
    top_all = functools.reduce(jnp.maximum, [s2[r, 0] for r in range(n_chip)])
    factors = [jnp.exp(s2[r, 0] - top_all) for r in range(n_chip)]
    grand = functools.reduce(jnp.add, [s2[r, 1] * factors[r] for r in range(n_chip)])
    wide[...] = jnp.zeros_like(wide)
    for r in range(n_chip):
        wide[r:r + 1, :] = factors[r] / grand
    tot[...] = jnp.transpose(wide[...])
    piece = core * n_chip + chip
    weight = tot[pl.ds(pl.multiple_of(piece * rows, rows), rows), :]
    mine_sum = snd2[chip].astype(F32) * weight[:, 0:1]
    for r in range(1, n_chip):
        second[r - 1].wait_recv()
        mine_sum = mine_sum + rcv2[r].astype(F32) * weight[:, r:r + 1]
    ag[piece] = mine_sum.astype(BF16)

    go(rcopy(ag.at[piece], ag.at[piece], sem_fw.at[0, 0], sem_fw.at[1, 0], partner))
    for r in range(1, n_chip):
        go(rcopy(ag.at[piece], ag.at[piece], sem_ag.at[0, r], sem_ag.at[1, r], peer(r)))
    win_in.wait()
    wout_in.wait()

    def expert(p):
        e = (p * rows) // slot_exp
        h = gelu_tanh(jnp.dot(ag[p], win[e], preferred_element_type=F32)).astype(BF16)
        return jnp.dot(h, wout[e], preferred_element_type=F32)

    def flush(rs):
        for r in rs:
            rcopy(snd3.at[r], rcv3.at[r], sem_3.at[0, r], sem_3.at[1, r], partner).wait_recv()
            y = (keep[r] + rcv3[r].astype(F32)).astype(BF16)
            for q in range(n_exp):
                snd4[r, q] = y[:, q * cols:(q + 1) * cols]
            for s in range(n_exp):
                if r or s:
                    go(rcopy(snd4.at[r, group_at(s)], rcv4.at[s, r], sem_4.at[0, s, r], sem_4.at[1, s, r], across(r, s)))

    group = 4
    ready = None
    for start in range(0, n_chip, group):
        rs = range(start, min(start + group, n_chip))
        for r in rs:
            p = core * n_chip + near(r)
            if r:
                rcopy(ag.at[p], ag.at[p], sem_ag.at[0, r], sem_ag.at[1, r], partner).wait_recv()
                go(rcopy(ag.at[p], ag.at[p], sem_fw.at[0, r], sem_fw.at[1, r], partner))
        for r in rs:
            keep[r] = expert(core * n_chip + near(r))
        for r in rs:
            p = other * n_chip + near(r)
            rcopy(ag.at[p], ag.at[p], sem_fw.at[0, r], sem_fw.at[1, r], partner).wait_recv()
        for r in rs:
            snd3[r] = expert(other * n_chip + near(r)).astype(BF16)
        for r in rs:
            go(rcopy(snd3.at[r], rcv3.at[r], sem_3.at[0, r], sem_3.at[1, r], partner))
        if ready is not None:
            flush(ready)
        ready = rs
    flush(ready)
    for s in range(n_exp):
        sums = snd4[0, mine].astype(F32) if s == 0 else None
        for r in range(n_chip):
            if r or s:
                rcopy(snd4.at[0, 0], rcv4.at[s, r], sem_4.at[0, s, r], sem_4.at[1, s, r], partner).wait_recv()
                got = rcv4[s, r].astype(F32)
                sums = got if sums is None else sums + got
        so[s, piece] = sums.astype(BF16)

    every = pl.ds(0, n_exp)

    def so_copy(p, sems, r, dev):
        return rcopy(so.at[every, p], so.at[every, p], sems.at[0, r], sems.at[1, r], dev)

    go(so_copy(piece, sem_af, 0, partner))
    for r in range(1, n_chip):
        go(so_copy(piece, sem_a, r, peer(r)))
    for r in range(1, n_chip):
        p = core * n_chip + near(r)
        so_copy(p, sem_a, r, partner).wait_recv()
        go(so_copy(p, sem_af, r, partner))
    for r in range(n_chip):
        so_copy(other * n_chip + near(r), sem_af, r, partner).wait_recv()
    so_out = pltpu.make_async_copy(so, so_hbm, sem_out.at[1])
    so_out.start()
    for cp in pending:
        cp.wait_send()
    comb_out.wait()
    so_out.wait()


def mix_kernel(comb, so, out):
    out[...] = jnp.dot(comb[...], so[...], preferred_element_type=F32).astype(BF16)


def mix(comb, so):
    count, slots = comb.shape
    cols = so.shape[1]
    step = next(s for s in (384, 256, 128, 64, 32, 16) if count % s == 0)
    return pl.pallas_call(
        mix_kernel,
        out_shape=jax.ShapeDtypeStruct((count, cols), BF16),
        grid=(count // step,),
        in_specs=[
            pl.BlockSpec((step, slots), lambda i: (i, 0)),
            pl.BlockSpec((slots, cols), lambda i: (0, 0)),
        ],
        out_specs=pl.BlockSpec((step, cols), lambda i: (i, 0)),
    )(comb, so)


def solution(mesh):
    n_seq, n_exp = mesh.shape["seq"], mesh.shape["exp"]
    n_chip = n_seq // 2

    def on_device(tokens, slot_embed, w_in, w_out):
        count, features = tokens.shape
        slots = slot_embed.shape[1]
        experts, _, hid = w_in.shape
        slot_exp = slots // experts
        rows = slots // n_seq
        half = slots // 2
        cols = features // n_exp
        n_tile = features // 256
        dma = pltpu.SemaphoreType.DMA
        vmem = pltpu.VMEM
        anywhere = pl.BlockSpec(memory_space=pl.ANY)
        comb, so = pl.pallas_call(
            functools.partial(kernel, n_seq, n_exp, slot_exp),
            out_shape=(
                jax.ShapeDtypeStruct((count, n_exp * slots), BF16),
                jax.ShapeDtypeStruct((n_exp, n_seq, rows, cols), BF16),
            ),
            in_specs=[anywhere] * 4,
            out_specs=(anywhere, anywhere),
            scratch_shapes=[
                vmem((count, features), BF16),
                vmem((n_exp, features, slots), BF16),
                vmem((slots, features), BF16),
                vmem(w_in.shape, BF16),
                vmem(w_out.shape, BF16),
                vmem((slots, count), F32),
                vmem((slots, count), BF16),
                vmem((slots, features), F32),
                vmem((count, n_exp * slots), BF16),
                vmem((2, 1, slots), F32),
                vmem((2, 1, slots), F32),
                vmem((n_chip, 2, 1, slots), F32),
                vmem((128, slots), F32),
                vmem((slots, 128), F32),
                vmem((n_tile, half, 256), BF16),
                vmem((n_tile, half, 256), BF16),
                vmem((n_chip, rows, features), BF16),
                vmem((n_chip, rows, features), BF16),
                vmem((n_seq, rows, features), BF16),
                vmem((n_chip, rows, features), F32),
                vmem((n_chip, rows, features), BF16),
                vmem((n_chip, rows, features), BF16),
                vmem((n_chip, n_exp, rows, cols), BF16),
                vmem((n_exp, n_chip, rows, cols), BF16),
                vmem((n_exp, n_seq, rows, cols), BF16),
                dma((-(-count // 512),)),
                dma,
                dma((2,)),
                dma((2,)),
                dma((2, n_exp)),
                dma((2, n_exp)),
                dma((2, 2)),
                dma((2, n_chip)),
                dma((2, n_tile)),
                dma((2, n_chip)),
                dma((2, n_chip)),
                dma((2, n_chip)),
                dma((2, n_chip)),
                dma((2, n_exp, n_chip)),
                dma((2, n_chip)),
                dma((2, n_chip)),
            ],
            compiler_params=pltpu.CompilerParams(
                collective_id=0, has_side_effects=True, vmem_limit_bytes=60 * 1024 * 1024
            ),
        )(tokens, slot_embed, w_in, w_out)
        so = so.reshape(n_exp * slots, cols)
        return mix(comb, so)

    placed = (P("seq", None), P(None, "exp"), P("exp", None, "seq"), P("exp", "seq", None))
    return jax.shard_map(
        on_device, mesh=mesh, in_specs=placed, out_specs=P("seq", "exp"), check_vma=False
    )
```

```python
import functools

import jax
import jax.numpy as jnp
from jax import lax
from jax.experimental import pallas as pl
from jax.experimental.pallas import tpu as pltpu
from jax.sharding import PartitionSpec as P

MESH = pl.DeviceIdType.MESH
F32 = jnp.float32
BF16 = jnp.bfloat16


def gelu_tanh(v):
    return 0.5 * v * (1.0 + jnp.tanh(0.7978845608028654 * (v + 0.044715 * v * v * v)))


def rcopy(src, dst, send, recv, dev):
    return pltpu.make_async_remote_copy(
        src_ref=src, dst_ref=dst, send_sem=send, recv_sem=recv, device_id=dev, device_id_type=MESH
    )


def column(row, slots):
    return jnp.transpose(jnp.broadcast_to(row, (128, slots)))


def kernel(
    n_seq, n_exp, slot_exp, tok_hbm, emb_hbm, win_hbm, wout_hbm, out,
    tok, emb, embt, win, wout, logt, pt, acc, comb, m1, l1, s2, wide, tot,
    snd1, rcv1, snd2, rcv2, ag, keep, snd3, rcv3, snd4, rcv4, so,
    sem_tok, sem_in, sem_w, sem_emb, sem_er, sem_m, sem_s,
    sem_1, sem_2, sem_ag, sem_fw, sem_3, sem_4, sem_a, sem_af,
):
    n_chip = n_seq // 2
    count, features = tok.shape
    slots = embt.shape[0]
    rows = slots // n_seq
    half = slots // 2
    cols = features // n_exp
    tile = 256
    n_tile = features // tile
    n_cut = so.shape[0]
    wide_cut = cols // n_cut
    me = lax.axis_index("seq")
    mine = lax.axis_index("exp")
    chip = me // 2
    core = lax.rem(me, 2)
    other = 1 - core
    partner = {"seq": chip * 2 + other}
    pending = []

    def near(r):
        return chip_ids[r]

    chip_ids = [chip]
    for r in range(1, n_chip):
        mate, bit = chip, 1
        while bit < n_chip:
            if r & bit:
                mate = mate + bit * (1 - 2 * lax.rem(chip // bit, 2))
            bit *= 2
        chip_ids.append(mate)

    def peer(r):
        return {"seq": near(r) * 2 + core}

    def group_at(s):
        return lax.rem(mine + s, n_exp)

    def across(r, s):
        return {"seq": near(r) * 2 + core, "exp": group_at(s)}

    def go(cp):
        cp.start()
        pending.append(cp)

    barrier = pltpu.get_barrier_semaphore()
    for s in range(n_exp):
        for r in range(n_chip):
            if r or s:
                pl.semaphore_signal(barrier, inc=1, device_id=across(r, s), device_id_type=MESH)
    pl.semaphore_signal(barrier, inc=1, device_id=partner, device_id_type=MESH)

    emb_in = pltpu.make_async_copy(emb_hbm, emb.at[0], sem_in)
    emb_in.start()
    chunks = []
    at = 0
    while at < count:
        size = min(512, count - at)
        cp = pltpu.make_async_copy(tok_hbm.at[pl.ds(at, size)], tok.at[pl.ds(at, size)], sem_tok.at[len(chunks)])
        cp.start()
        chunks.append((at, size, cp))
        at += size

    emb_in.wait()
    for q in range(n_tile):
        embt[:, q * tile:(q + 1) * tile] = jnp.transpose(emb[0, q * tile:(q + 1) * tile, :])
    peak = None
    deep = features // 2

    def part_of(which):
        return pl.ds(pl.multiple_of(which * deep, deep), deep)

    def emb_copy(r):
        there = emb.at[r, part_of(core)]
        return rcopy(emb.at[0, part_of(core)], there, sem_emb.at[0, r], sem_emb.at[1, r], {"exp": group_at(r)})

    def emb_relay(r, which):
        there = emb.at[r, part_of(which)]
        return rcopy(there, there, sem_er.at[0, r], sem_er.at[1, r], partner)

    for at, size, cp in chunks:
        cp.wait()
        lt = lax.dot_general(
            embt[...], tok[at:at + size, :], (((1,), (1,)), ((), ())), preferred_element_type=F32
        )
        logt[:, at:at + size] = lt
        top = jnp.max(lt, axis=1, keepdims=True)
        peak = top if peak is None else jnp.maximum(peak, top)
        if at == 0:
            pl.semaphore_wait(barrier, n_chip * n_exp)
            for r in range(1, n_exp):
                go(emb_copy(r))
    win_in = pltpu.make_async_copy(win_hbm, win, sem_w.at[0])
    wout_in = pltpu.make_async_copy(wout_hbm, wout, sem_w.at[1])
    win_in.start()
    wout_in.start()
    m1[0] = jnp.transpose(jnp.broadcast_to(peak, (slots, 128)))[0:1, :]
    m_copy = rcopy(m1.at[0], m1.at[1], sem_m.at[0, 0], sem_m.at[1, 0], partner)
    go(m_copy)

    total = None
    for at, size, _ in chunks:
        w = jnp.exp(logt[:, at:at + size] - peak)
        pt[:, at:at + size] = w.astype(BF16)
        part = jnp.sum(w, axis=1, keepdims=True)
        total = part if total is None else total + part
    l1[0] = jnp.transpose(jnp.broadcast_to(total, (slots, 128)))[0:1, :]
    l_copy = rcopy(l1.at[0], l1.at[1], sem_m.at[0, 1], sem_m.at[1, 1], partner)
    go(l_copy)

    m_copy.wait_recv()
    top_pair = jnp.maximum(m1[0], m1[1])
    scale = column(jnp.exp(m1[0] - top_pair), slots)[:, 0:1]

    def half_rows(which):
        return pl.ds(pl.multiple_of(which * half, half), half)

    first = []
    for q in range(n_tile):
        acc[:, q * tile:(q + 1) * tile] = scale * jnp.dot(
            pt[...], tok[:, q * tile:(q + 1) * tile], preferred_element_type=F32
        )
        snd1[q] = acc[half_rows(other), q * tile:(q + 1) * tile].astype(BF16)
        cp = rcopy(snd1.at[q], rcv1.at[q], sem_1.at[0, q], sem_1.at[1, q], partner)
        go(cp)
        first.append(cp)
    l_copy.wait_recv()
    s2[0, 0] = top_pair
    s2[0, 1] = l1[0] * jnp.exp(m1[0] - top_pair) + l1[1] * jnp.exp(m1[1] - top_pair)
    stats = [rcopy(s2.at[0], s2.at[r], sem_s.at[0, r], sem_s.at[1, r], peer(r)) for r in range(1, n_chip)]
    for cp in stats:
        go(cp)
    for q in range(n_tile):
        first[q].wait_recv()
        both = acc[half_rows(core), q * tile:(q + 1) * tile] + rcv1[q].astype(F32)
        snd2[:, :, q * tile:(q + 1) * tile] = both.reshape(n_chip, rows, tile).astype(BF16)
    second = []
    for r in range(1, n_chip):
        cp = rcopy(snd2.at[near(r)], rcv2.at[r], sem_2.at[0, r], sem_2.at[1, r], peer(r))
        go(cp)
        second.append(cp)

    for r in range(1, n_exp):
        emb_copy(r).wait_recv()
        go(emb_relay(r, core))
    for r in range(1, n_exp):
        emb_relay(r, other).wait_recv()
    step = next(s for s in (384, 256, 128, 64, 32, 16) if count % s == 0)

    def combine(i, carry):
        here = pl.ds(pl.multiple_of(i * step, step), step)
        rows_in = tok[here, :]
        parts = [jnp.dot(rows_in, emb[r], preferred_element_type=F32) for r in range(n_exp)]
        top = jnp.max(functools.reduce(jnp.maximum, parts), axis=1, keepdims=True)
        parts = [jnp.exp(v - top) for v in parts]
        full = jnp.sum(functools.reduce(jnp.add, parts), axis=1, keepdims=True)
        inv = 1.0 / full
        for r in range(n_exp):
            comb[here, r * slots:(r + 1) * slots] = (parts[r] * inv).astype(BF16)
        return carry

    lax.fori_loop(0, count // step, combine, 0)

    for cp in stats:
        cp.wait_recv()
    top_all = functools.reduce(jnp.maximum, [s2[r, 0] for r in range(n_chip)])
    factors = [jnp.exp(s2[r, 0] - top_all) for r in range(n_chip)]
    grand = functools.reduce(jnp.add, [s2[r, 1] * factors[r] for r in range(n_chip)])
    wide[...] = jnp.zeros_like(wide)
    for r in range(n_chip):
        wide[r:r + 1, :] = factors[r] / grand
    tot[...] = jnp.transpose(wide[...])
    piece = core * n_chip + chip
    weight = tot[pl.ds(pl.multiple_of(piece * rows, rows), rows), :]
    mine_sum = snd2[chip].astype(F32) * weight[:, 0:1]
    for r in range(1, n_chip):
        second[r - 1].wait_recv()
        mine_sum = mine_sum + rcv2[r].astype(F32) * weight[:, r:r + 1]
    ag[piece] = mine_sum.astype(BF16)

    go(rcopy(ag.at[piece], ag.at[piece], sem_fw.at[0, 0], sem_fw.at[1, 0], partner))
    for r in range(1, n_chip):
        go(rcopy(ag.at[piece], ag.at[piece], sem_ag.at[0, r], sem_ag.at[1, r], peer(r)))
    win_in.wait()
    wout_in.wait()

    def expert(p):
        e = (p * rows) // slot_exp
        h = gelu_tanh(jnp.dot(ag[p], win[e], preferred_element_type=F32)).astype(BF16)
        return jnp.dot(h, wout[e], preferred_element_type=F32)

    def mix_copy(h, s, r, dev):
        return rcopy(
            snd4.at[r, group_at(s), h], rcv4.at[h, s, r], sem_4.at[0, h, s, r], sem_4.at[1, h, s, r], dev
        )

    def flush(rs):
        for r in rs:
            rcopy(snd3.at[r], rcv3.at[r], sem_3.at[0, r], sem_3.at[1, r], partner).wait_recv()
            y = (keep[r] + rcv3[r].astype(F32)).astype(BF16)
            for q in range(n_exp):
                for h in range(n_cut):
                    low = q * cols + h * wide_cut
                    snd4[r, q, h] = y[:, low:low + wide_cut]
            for s in range(n_exp):
                if r or s:
                    go(mix_copy(0, s, r, across(r, s)))
        for h in range(1, n_cut):
            for r in rs:
                for s in range(n_exp):
                    if r or s:
                        go(mix_copy(h, s, r, across(r, s)))

    group = 4
    ready = None
    for start in range(0, n_chip, group):
        rs = range(start, min(start + group, n_chip))
        for r in rs:
            p = core * n_chip + near(r)
            if r:
                rcopy(ag.at[p], ag.at[p], sem_ag.at[0, r], sem_ag.at[1, r], partner).wait_recv()
                go(rcopy(ag.at[p], ag.at[p], sem_fw.at[0, r], sem_fw.at[1, r], partner))
        for r in rs:
            keep[r] = expert(core * n_chip + near(r))
        for r in rs:
            p = other * n_chip + near(r)
            rcopy(ag.at[p], ag.at[p], sem_fw.at[0, r], sem_fw.at[1, r], partner).wait_recv()
        for r in rs:
            snd3[r] = expert(other * n_chip + near(r)).astype(BF16)
        for r in rs:
            go(rcopy(snd3.at[r], rcv3.at[r], sem_3.at[0, r], sem_3.at[1, r], partner))
        if ready is not None:
            flush(ready)
        ready = rs
    flush(ready)
    every = pl.ds(0, n_exp)

    def so_copy(h, p, sems, r, dev):
        span = so.at[h, every, p]
        return rcopy(span, span, sems.at[0, h, r], sems.at[1, h, r], dev)

    for h in range(n_cut):
        for s in range(n_exp):
            sums = snd4[0, mine, h].astype(F32) if s == 0 else None
            for r in range(n_chip):
                if r or s:
                    mix_copy(h, s, r, partner).wait_recv()
                    got = rcv4[h, s, r].astype(F32)
                    sums = got if sums is None else sums + got
            so[h, s, piece] = sums.astype(BF16)
        go(so_copy(h, piece, sem_af, 0, partner))
        for r in range(1, n_chip):
            go(so_copy(h, piece, sem_a, r, peer(r)))
    for h in range(n_cut):
        for r in range(1, n_chip):
            p = core * n_chip + near(r)
            so_copy(h, p, sem_a, r, partner).wait_recv()
            go(so_copy(h, p, sem_af, r, partner))
    flat = (n_exp * slots, wide_cut)
    for h in range(n_cut):
        for r in range(n_chip):
            so_copy(h, other * n_chip + near(r), sem_af, r, partner).wait_recv()
        for i in range(count // step):
            here = pl.ds(i * step, step)
            table = so[h].reshape(flat) if rows % 16 == 0 else so[h].astype(F32).reshape(flat).astype(BF16)
            mixed = jnp.dot(comb[here, :], table, preferred_element_type=F32).astype(BF16)
            out[here, h * wide_cut:(h + 1) * wide_cut] = mixed
    for cp in pending:
        cp.wait_send()


def solution(mesh):
    n_seq, n_exp = mesh.shape["seq"], mesh.shape["exp"]
    n_chip = n_seq // 2

    def on_device(tokens, slot_embed, w_in, w_out):
        count, features = tokens.shape
        slots = slot_embed.shape[1]
        experts, _, hid = w_in.shape
        slot_exp = slots // experts
        rows = slots // n_seq
        half = slots // 2
        cols = features // n_exp
        n_tile = features // 256
        n_cut = 2 if cols % 256 == 0 else 1
        dma = pltpu.SemaphoreType.DMA
        vmem = pltpu.VMEM
        anywhere = pl.BlockSpec(memory_space=pltpu.HBM)
        return pl.pallas_call(
            functools.partial(kernel, n_seq, n_exp, slot_exp),
            out_shape=jax.ShapeDtypeStruct((count, cols), BF16),
            in_specs=[anywhere] * 4,
            out_specs=pl.BlockSpec(memory_space=pltpu.VMEM),
            scratch_shapes=[
                vmem((count, features), BF16),
                vmem((n_exp, features, slots), BF16),
                vmem((slots, features), BF16),
                vmem(w_in.shape, BF16),
                vmem(w_out.shape, BF16),
                vmem((slots, count), F32),
                vmem((slots, count), BF16),
                vmem((slots, features), F32),
                vmem((count, n_exp * slots), BF16),
                vmem((2, 1, slots), F32),
                vmem((2, 1, slots), F32),
                vmem((n_chip, 2, 1, slots), F32),
                vmem((128, slots), F32),
                vmem((slots, 128), F32),
                vmem((n_tile, half, 256), BF16),
                vmem((n_tile, half, 256), BF16),
                vmem((n_chip, rows, features), BF16),
                vmem((n_chip, rows, features), BF16),
                vmem((n_seq, rows, features), BF16),
                vmem((n_chip, rows, features), F32),
                vmem((n_chip, rows, features), BF16),
                vmem((n_chip, rows, features), BF16),
                vmem((n_chip, n_exp, n_cut, rows, cols // n_cut), BF16),
                vmem((n_cut, n_exp, n_chip, rows, cols // n_cut), BF16),
                vmem((n_cut, n_exp, n_seq, rows, cols // n_cut), BF16),
                dma((-(-count // 512),)),
                dma,
                dma((2,)),
                dma((2, n_exp)),
                dma((2, n_exp)),
                dma((2, 2)),
                dma((2, n_chip)),
                dma((2, n_tile)),
                dma((2, n_chip)),
                dma((2, n_chip)),
                dma((2, n_chip)),
                dma((2, n_chip)),
                dma((2, n_cut, n_exp, n_chip)),
                dma((2, n_cut, n_chip)),
                dma((2, n_cut, n_chip)),
            ],
            compiler_params=pltpu.CompilerParams(
                collective_id=0, has_side_effects=True, vmem_limit_bytes=49 * 1024 * 1024
            ),
        )(tokens, slot_embed, w_in, w_out)

    placed = (P("seq", None), P(None, "exp"), P("exp", None, "seq"), P("exp", "seq", None))
    return jax.shard_map(
        on_device, mesh=mesh, in_specs=placed, out_specs=P("seq", "exp"), check_vma=False
    )
```

```python
import functools

import jax
import jax.numpy as jnp
from jax import lax
from jax.experimental import pallas as pl
from jax.experimental.pallas import tpu as pltpu
from jax.sharding import PartitionSpec as P

MESH = pl.DeviceIdType.MESH
F32 = jnp.float32
BF16 = jnp.bfloat16


def gelu_tanh(v):
    return 0.5 * v * (1.0 + jnp.tanh(0.7978845608028654 * (v + 0.044715 * v * v * v)))


def rcopy(src, dst, send, recv, dev):
    return pltpu.make_async_remote_copy(
        src_ref=src, dst_ref=dst, send_sem=send, recv_sem=recv, device_id=dev, device_id_type=MESH
    )


def column(row, slots):
    return jnp.transpose(jnp.broadcast_to(row, (128, slots)))


def kernel(
    n_seq, n_exp, slot_exp, tok_hbm, emb_hbm, win_hbm, wout_hbm, out,
    tok, emb, embt, win, wout, logt, pt, acc, comb, m1, l1, s2, wide, tot,
    snd1, rcv1, snd2, rcv2, ag, keep, snd3, rcv3, snd4, rcv4, so,
    sem_tok, sem_in, sem_w, sem_emb, sem_er, sem_m, sem_s,
    sem_1, sem_2, sem_ag, sem_fw, sem_3, sem_4, sem_a, sem_af,
):
    n_chip = n_seq // 2
    count, features = tok.shape
    slots = embt.shape[0]
    rows = slots // n_seq
    half = slots // 2
    cols = features // n_exp
    tile = 256
    n_tile = features // tile
    n_cut = so.shape[0]
    wide_cut = cols // n_cut
    me = lax.axis_index("seq")
    mine = lax.axis_index("exp")
    chip = me // 2
    core = lax.rem(me, 2)
    other = 1 - core
    partner = {"seq": chip * 2 + other}
    pending = []

    def near(r):
        return chip_ids[r]

    chip_ids = [chip]
    for r in range(1, n_chip):
        mate, bit = chip, 1
        while bit < n_chip:
            if r & bit:
                mate = mate + bit * (1 - 2 * lax.rem(chip // bit, 2))
            bit *= 2
        chip_ids.append(mate)

    def peer(r):
        return {"seq": near(r) * 2 + core}

    def group_at(s):
        return lax.rem(mine + s, n_exp)

    def across(r, s):
        return {"seq": near(r) * 2 + core, "exp": group_at(s)}

    def go(cp):
        cp.start()
        pending.append(cp)

    barrier = pltpu.get_barrier_semaphore()
    for s in range(n_exp):
        for r in range(n_chip):
            if r or s:
                pl.semaphore_signal(barrier, inc=1, device_id=across(r, s), device_id_type=MESH)
    pl.semaphore_signal(barrier, inc=1, device_id=partner, device_id_type=MESH)

    emb_in = pltpu.make_async_copy(emb_hbm, emb.at[0], sem_in)
    emb_in.start()
    chunks = []
    at = 0
    while at < count:
        size = min(512, count - at)
        cp = pltpu.make_async_copy(tok_hbm.at[pl.ds(at, size)], tok.at[pl.ds(at, size)], sem_tok.at[len(chunks)])
        cp.start()
        chunks.append((at, size, cp))
        at += size

    emb_in.wait()
    for q in range(n_tile):
        embt[:, q * tile:(q + 1) * tile] = jnp.transpose(emb[0, q * tile:(q + 1) * tile, :])
    peak = None
    deep = features // 2

    def part_of(which):
        return pl.ds(pl.multiple_of(which * deep, deep), deep)

    def emb_copy(r):
        there = emb.at[r, part_of(core)]
        return rcopy(emb.at[0, part_of(core)], there, sem_emb.at[0, r], sem_emb.at[1, r], {"exp": group_at(r)})

    def emb_relay(r, which):
        there = emb.at[r, part_of(which)]
        return rcopy(there, there, sem_er.at[0, r], sem_er.at[1, r], partner)

    for at, size, cp in chunks:
        cp.wait()
        lt = lax.dot_general(
            embt[...], tok[at:at + size, :], (((1,), (1,)), ((), ())), preferred_element_type=F32
        )
        logt[:, at:at + size] = lt
        top = jnp.max(lt, axis=1, keepdims=True)
        peak = top if peak is None else jnp.maximum(peak, top)
        if at == 0:
            pl.semaphore_wait(barrier, n_chip * n_exp)
            for r in range(1, n_exp):
                go(emb_copy(r))
    win_in = pltpu.make_async_copy(win_hbm, win, sem_w.at[0])
    wout_in = pltpu.make_async_copy(wout_hbm, wout, sem_w.at[1])
    win_in.start()
    wout_in.start()
    m1[0] = jnp.transpose(jnp.broadcast_to(peak, (slots, 128)))[0:1, :]
    m_copy = rcopy(m1.at[0], m1.at[1], sem_m.at[0, 0], sem_m.at[1, 0], partner)
    go(m_copy)

    total = None
    for at, size, _ in chunks:
        w = jnp.exp(logt[:, at:at + size] - peak)
        pt[:, at:at + size] = w.astype(BF16)
        part = jnp.sum(w, axis=1, keepdims=True)
        total = part if total is None else total + part
    l1[0] = jnp.transpose(jnp.broadcast_to(total, (slots, 128)))[0:1, :]
    l_copy = rcopy(l1.at[0], l1.at[1], sem_m.at[0, 1], sem_m.at[1, 1], partner)
    go(l_copy)

    m_copy.wait_recv()
    top_pair = jnp.maximum(m1[0], m1[1])
    scale = column(jnp.exp(m1[0] - top_pair), slots)[:, 0:1]

    def half_rows(which):
        return pl.ds(pl.multiple_of(which * half, half), half)

    first = []
    for q in range(n_tile):
        acc[:, q * tile:(q + 1) * tile] = scale * jnp.dot(
            pt[...], tok[:, q * tile:(q + 1) * tile], preferred_element_type=F32
        )
        snd1[q] = acc[half_rows(other), q * tile:(q + 1) * tile].astype(BF16)
        cp = rcopy(snd1.at[q], rcv1.at[q], sem_1.at[0, q], sem_1.at[1, q], partner)
        go(cp)
        first.append(cp)
    l_copy.wait_recv()
    s2[0, 0] = top_pair
    s2[0, 1] = l1[0] * jnp.exp(m1[0] - top_pair) + l1[1] * jnp.exp(m1[1] - top_pair)
    stats = [rcopy(s2.at[0], s2.at[r], sem_s.at[0, r], sem_s.at[1, r], peer(r)) for r in range(1, n_chip)]
    for cp in stats:
        go(cp)
    for q in range(n_tile):
        first[q].wait_recv()
        both = acc[half_rows(core), q * tile:(q + 1) * tile] + rcv1[q].astype(F32)
        snd2[:, :, q * tile:(q + 1) * tile] = both.reshape(n_chip, rows, tile).astype(BF16)
    second = []
    for r in range(1, n_chip):
        cp = rcopy(snd2.at[near(r)], rcv2.at[r], sem_2.at[0, r], sem_2.at[1, r], peer(r))
        go(cp)
        second.append(cp)

    for r in range(1, n_exp):
        emb_copy(r).wait_recv()
        go(emb_relay(r, core))
    for r in range(1, n_exp):
        emb_relay(r, other).wait_recv()
    step = next(s for s in (384, 256, 128, 64, 32, 16) if count % s == 0)

    def combine(i, carry):
        here = pl.ds(pl.multiple_of(i * step, step), step)
        rows_in = tok[here, :]
        parts = [jnp.dot(rows_in, emb[r], preferred_element_type=F32) for r in range(n_exp)]
        top = jnp.max(functools.reduce(jnp.maximum, parts), axis=1, keepdims=True)
        parts = [jnp.exp(v - top) for v in parts]
        full = jnp.sum(functools.reduce(jnp.add, parts), axis=1, keepdims=True)
        inv = 1.0 / full
        for r in range(n_exp):
            comb[here, r * slots:(r + 1) * slots] = (parts[r] * inv).astype(BF16)
        return carry

    lax.fori_loop(0, count // step, combine, 0)

    for cp in stats:
        cp.wait_recv()
    top_all = functools.reduce(jnp.maximum, [s2[r, 0] for r in range(n_chip)])
    factors = [jnp.exp(s2[r, 0] - top_all) for r in range(n_chip)]
    grand = functools.reduce(jnp.add, [s2[r, 1] * factors[r] for r in range(n_chip)])
    wide[...] = jnp.zeros_like(wide)
    for r in range(n_chip):
        wide[r:r + 1, :] = factors[r] / grand
    tot[...] = jnp.transpose(wide[...])
    piece = core * n_chip + chip
    weight = tot[pl.ds(pl.multiple_of(piece * rows, rows), rows), :]
    mine_sum = snd2[chip].astype(F32) * weight[:, 0:1]
    for r in range(1, n_chip):
        second[r - 1].wait_recv()
        mine_sum = mine_sum + rcv2[r].astype(F32) * weight[:, r:r + 1]
    ag[piece] = mine_sum.astype(BF16)

    go(rcopy(ag.at[piece], ag.at[piece], sem_fw.at[0, 0], sem_fw.at[1, 0], partner))
    for r in range(1, n_chip):
        go(rcopy(ag.at[piece], ag.at[piece], sem_ag.at[0, r], sem_ag.at[1, r], peer(r)))
    win_in.wait()
    wout_in.wait()

    def expert(p):
        e = (p * rows) // slot_exp
        h = gelu_tanh(jnp.dot(ag[p], win[e], preferred_element_type=F32)).astype(BF16)
        return jnp.dot(h, wout[e], preferred_element_type=F32)

    def mix_copy(h, s, r, dev):
        return rcopy(
            snd4.at[r, group_at(s), h], rcv4.at[h, s, r], sem_4.at[0, h, s, r], sem_4.at[1, h, s, r], dev
        )

    def flush(rs):
        for r in rs:
            rcopy(snd3.at[r], rcv3.at[r], sem_3.at[0, r], sem_3.at[1, r], partner).wait_recv()
            y = (keep[r] + rcv3[r].astype(F32)).astype(BF16)
            for q in range(n_exp):
                for h in range(n_cut):
                    low = q * cols + h * wide_cut
                    snd4[r, q, h] = y[:, low:low + wide_cut]
            for s in range(n_exp):
                if r or s:
                    go(mix_copy(0, s, r, across(r, s)))
        for h in range(1, n_cut):
            for r in rs:
                for s in range(n_exp):
                    if r or s:
                        go(mix_copy(h, s, r, across(r, s)))

    group = 2
    ready = None
    for start in range(0, n_chip, group):
        rs = range(start, min(start + group, n_chip))
        for r in rs:
            p = core * n_chip + near(r)
            if r:
                rcopy(ag.at[p], ag.at[p], sem_ag.at[0, r], sem_ag.at[1, r], partner).wait_recv()
                go(rcopy(ag.at[p], ag.at[p], sem_fw.at[0, r], sem_fw.at[1, r], partner))
        for r in rs:
            keep[r] = expert(core * n_chip + near(r))
        for r in rs:
            p = other * n_chip + near(r)
            rcopy(ag.at[p], ag.at[p], sem_fw.at[0, r], sem_fw.at[1, r], partner).wait_recv()
        for r in rs:
            snd3[r] = expert(other * n_chip + near(r)).astype(BF16)
        for r in rs:
            go(rcopy(snd3.at[r], rcv3.at[r], sem_3.at[0, r], sem_3.at[1, r], partner))
        if ready is not None:
            flush(ready)
        ready = rs
    flush(ready)
    every = pl.ds(0, n_exp)

    def so_copy(h, p, sems, r, dev):
        span = so.at[h, every, p]
        return rcopy(span, span, sems.at[0, h, r], sems.at[1, h, r], dev)

    for h in range(n_cut):
        for s in range(n_exp):
            sums = snd4[0, mine, h].astype(F32) if s == 0 else None
            for r in range(n_chip):
                if r or s:
                    mix_copy(h, s, r, partner).wait_recv()
                    got = rcv4[h, s, r].astype(F32)
                    sums = got if sums is None else sums + got
            so[h, s, piece] = sums.astype(BF16)
        go(so_copy(h, piece, sem_af, 0, partner))
        for r in range(1, n_chip):
            go(so_copy(h, piece, sem_a, r, peer(r)))
    for h in range(n_cut):
        for r in range(1, n_chip):
            p = core * n_chip + near(r)
            so_copy(h, p, sem_a, r, partner).wait_recv()
            go(so_copy(h, p, sem_af, r, partner))
    flat = (n_exp * slots, wide_cut)
    for h in range(n_cut):
        for r in range(n_chip):
            so_copy(h, other * n_chip + near(r), sem_af, r, partner).wait_recv()
        for i in range(count // step):
            here = pl.ds(i * step, step)
            table = so[h].reshape(flat) if rows % 16 == 0 else so[h].astype(F32).reshape(flat).astype(BF16)
            mixed = jnp.dot(comb[here, :], table, preferred_element_type=F32).astype(BF16)
            out[here, h * wide_cut:(h + 1) * wide_cut] = mixed
    for cp in pending:
        cp.wait_send()


def solution(mesh):
    n_seq, n_exp = mesh.shape["seq"], mesh.shape["exp"]
    n_chip = n_seq // 2

    def on_device(tokens, slot_embed, w_in, w_out):
        count, features = tokens.shape
        slots = slot_embed.shape[1]
        experts, _, hid = w_in.shape
        slot_exp = slots // experts
        rows = slots // n_seq
        half = slots // 2
        cols = features // n_exp
        n_tile = features // 256
        n_cut = 2 if cols % 256 == 0 else 1
        dma = pltpu.SemaphoreType.DMA
        vmem = pltpu.VMEM
        anywhere = pl.BlockSpec(memory_space=pltpu.HBM)
        return pl.pallas_call(
            functools.partial(kernel, n_seq, n_exp, slot_exp),
            out_shape=jax.ShapeDtypeStruct((count, cols), BF16),
            in_specs=[anywhere] * 4,
            out_specs=pl.BlockSpec(memory_space=pltpu.VMEM),
            scratch_shapes=[
                vmem((count, features), BF16),
                vmem((n_exp, features, slots), BF16),
                vmem((slots, features), BF16),
                vmem(w_in.shape, BF16),
                vmem(w_out.shape, BF16),
                vmem((slots, count), F32),
                vmem((slots, count), BF16),
                vmem((slots, features), F32),
                vmem((count, n_exp * slots), BF16),
                vmem((2, 1, slots), F32),
                vmem((2, 1, slots), F32),
                vmem((n_chip, 2, 1, slots), F32),
                vmem((128, slots), F32),
                vmem((slots, 128), F32),
                vmem((n_tile, half, 256), BF16),
                vmem((n_tile, half, 256), BF16),
                vmem((n_chip, rows, features), BF16),
                vmem((n_chip, rows, features), BF16),
                vmem((n_seq, rows, features), BF16),
                vmem((n_chip, rows, features), F32),
                vmem((n_chip, rows, features), BF16),
                vmem((n_chip, rows, features), BF16),
                vmem((n_chip, n_exp, n_cut, rows, cols // n_cut), BF16),
                vmem((n_cut, n_exp, n_chip, rows, cols // n_cut), BF16),
                vmem((n_cut, n_exp, n_seq, rows, cols // n_cut), BF16),
                dma((-(-count // 512),)),
                dma,
                dma((2,)),
                dma((2, n_exp)),
                dma((2, n_exp)),
                dma((2, 2)),
                dma((2, n_chip)),
                dma((2, n_tile)),
                dma((2, n_chip)),
                dma((2, n_chip)),
                dma((2, n_chip)),
                dma((2, n_chip)),
                dma((2, n_cut, n_exp, n_chip)),
                dma((2, n_cut, n_chip)),
                dma((2, n_cut, n_chip)),
            ],
            compiler_params=pltpu.CompilerParams(
                collective_id=0, has_side_effects=True, vmem_limit_bytes=49 * 1024 * 1024
            ),
        )(tokens, slot_embed, w_in, w_out)

    placed = (P("seq", None), P(None, "exp"), P("exp", None, "seq"), P("exp", "seq", None))
    return jax.shard_map(
        on_device, mesh=mesh, in_specs=placed, out_specs=P("seq", "exp"), check_vma=False
    )
```
